32 devices in a mesh: tm: 4 (over x, core), cell: 8 (over z, y).
Axes of the slice: x: 2, y: 2, z: 4, core: 2. Of those that a mesh axis runs over, the one named last changes fastest.
Arguments:
- sensitivity: bfloat16 [2048, 4, 4096], P(None, 'tm', 'cell'), may hold values from -0.1875 to 0.1875
- duals: bfloat16 [2048, 128], P(('tm', 'cell')), may hold values from -6 to 6
- time_cov: float32 [4, 4], replicated, may hold values from 0.05 to 0.5
- cell_coords: int32 [2, 4096], P(None, 'cell'), may hold values from 0 to 127, as said below
- obs_time: int32 [2048], replicated, may hold values from 0 to 3
- obs_owner: int32 [2048], replicated, may hold values from 0 to 2047, each once
Outputs:
- product: float32 [2048, 128], P(('tm', 'cell'))
The draws below stay inside these ranges and needn't reach their ends.
Inputs may be any that keep to these rules, and one draw needn't show every extreme that they name: `cell_coords`: every cell has its own grid position; rows lie below 32 and columns below 128. `obs_owner`: every observation stands in exactly one slot.
All inputs are finite; a program needn't handle non-finite values.
Results may differ from the reference program's by a relative error of at most 0.0049.
Values may be sent and summed in bfloat16 or wider, within the bound.
A program may use at most 64 MiB of HBM per device.

```python
import jax
import jax.numpy as jnp
from jax import lax

OBS = 2048
REALS = 128
GRID_COLS = 128
LSCALE = 4
TIMES = 4
CELLS = 4096


def draw_cell_coords(key, part):
    placed = jax.random.permutation(jax.random.fold_in(key, 17), CELLS).astype(jnp.int32)
    return jnp.stack([placed // GRID_COLS, placed % GRID_COLS]).astype(jnp.int32)


def plant(drawn, stream_key, low, largest):
    longest = drawn.shape.index(max(drawn.shape))
    spots = []
    for shift in (0, 1):
        where = [jax.random.randint(jax.random.fold_in(stream_key, axis), (), 0, length) for axis, length in enumerate(drawn.shape)]
        where[longest] = (where[longest] + shift) % drawn.shape[longest]
        spots.append(tuple(where))
    return drawn.at[spots[0]].set(low).at[spots[1]].set(largest)


def raised(array, stream_key, source, target, blocks, factor):
    owner, partner = [(jnp.arange(array.shape[axis_at]) // (array.shape[axis_at] // blocks)).reshape([-1 if axis == axis_at else 1 for axis in range(array.ndim)]) for axis_at in (source, target)]
    chosen = jax.random.permutation(stream_key, blocks)[partner]
    strong = (owner == chosen) | (owner == (partner + blocks // 2) % blocks)
    return jnp.where(strong, factor * array, array)


def levels(own_key, shape, cuts, least, high):
    def one(dim, parts):
        draws = jax.random.uniform(jax.random.fold_in(jax.random.fold_in(own_key, 6), dim), (parts,), jnp.float32, least / len(cuts), high / len(cuts))
        return jnp.repeat(jnp.exp(draws), shape[dim] // parts).reshape((-1,) + (1,) * (len(shape) - dim - 1))

    gain = one(*cuts[0])
    for cut in cuts[1:]:
        gain = gain * one(*cut)
    return gain


def normal_values(stream_key, shape, deviation, limit, cuts=(), kind=jnp.bfloat16):
    drawn = jax.random.normal(stream_key, shape, jnp.float32) * deviation
    if len(cuts) > 0:
        drawn = levels(stream_key, shape, cuts, -0.22, 0.18) * drawn
    return jnp.clip(drawn, min=-limit, max=limit).astype(kind)


def gaussian_with(key, dims, scale, reach, shards, heavy, kind=jnp.bfloat16):
    array = scale * jax.random.normal(key, dims, jnp.float32)
    if shards:
        array = array * levels(key, dims, shards, -0.22, 0.18)
    return jnp.clip(raised(array, jax.random.fold_in(key, 3), *heavy), -reach, reach).astype(kind)


def setup_inputs(seed: int = 0) -> dict:
    splits = jax.random.split(jax.random.key(seed), 7)
    return {
        "sensitivity": gaussian_with(splits[0], (OBS, TIMES, CELLS), OBS ** -0.5, 0.1875, ((1, 4), (2, 8)), (2, 0, 8, 2.0)),
        "duals": normal_values(splits[1], (OBS, REALS), 1.0, 6.0, ((0, 32),)),
        "time_cov": jnp.clip(jax.random.uniform(splits[2], (TIMES, TIMES), jnp.float32, 0.05, 0.5), 0.05, 0.5),
        "cell_coords": draw_cell_coords(jax.random.fold_in(splits[6], 71), 0),
        "obs_time": plant(jax.random.randint(splits[4], (OBS,), 0, TIMES), jax.random.fold_in(splits[4], 1), 0, TIMES - 1).astype(jnp.int32),
        "obs_owner": jax.random.permutation(splits[5], OBS).astype(jnp.int32),
    }


def covariance(left_coords, right_coords):
    row_gap = (left_coords[0][:, None] - right_coords[0][None, :]).astype(jnp.float32)
    col_gap = (left_coords[1][:, None] - right_coords[1][None, :]).astype(jnp.float32)
    distance = jnp.sqrt(row_gap * row_gap + col_gap * col_gap)
    return (jnp.exp(-distance / LSCALE) / (8.0 * LSCALE)).astype(jnp.bfloat16)

def reference(sensitivity, duals, time_cov, cell_coords, obs_time, obs_owner):
    time_index = jnp.arange(TIMES, dtype=jnp.int32)
    live = time_index[None, :, None] <= obs_time[:, None, None]
    masked = jnp.where(live, sensitivity, jnp.zeros((), jnp.bfloat16))
    flattened = masked.reshape(OBS, TIMES * CELLS)
    adjoint = jnp.dot(flattened.T, duals, preferred_element_type=jnp.float32).astype(jnp.bfloat16)
    adjoint_f = adjoint.reshape(TIMES, CELLS, REALS).astype(jnp.float32)
    mixed = jnp.einsum('st,tcr->scr', time_cov, adjoint_f, precision=lax.Precision.HIGHEST).astype(jnp.bfloat16)
    columns = mixed.transpose(1, 0, 2).reshape(CELLS, TIMES * REALS)
    width = min(512, CELLS)
    starts = jnp.arange(0, CELLS, width, dtype=jnp.int32)

    def row_block(offset):
        left_coords = lax.dynamic_slice_in_dim(cell_coords, offset, width, 1)
        kernel = covariance(left_coords, cell_coords)
        return jnp.dot(kernel, columns, preferred_element_type=jnp.float32).astype(jnp.bfloat16)
    weighted = lax.map(row_block, starts).reshape(CELLS, TIMES, REALS)
    weighted_flat = weighted.transpose(1, 0, 2).reshape(TIMES * CELLS, REALS)
    forward = jnp.dot(flattened, weighted_flat, preferred_element_type=jnp.float32)
    return forward[obs_owner]
```

```python
import functools

import jax
import jax.numpy as jnp
from jax import lax
from jax.experimental import pallas as pl
from jax.experimental.pallas import tpu as pltpu
from jax.sharding import PartitionSpec as P

LSCALE = 4
LANES = 128
HALVES = 2
PICK_ROWS = 256
MESH = pl.DeviceIdType.MESH
BF16 = jnp.bfloat16
F32 = jnp.float32


def remote(src, dst, sems, index, device):
    send, recv = sems
    return pltpu.make_async_remote_copy(
        src_ref=src, dst_ref=dst, send_sem=send.at[index], recv_sem=recv.at[index],
        device_id=device, device_id_type=MESH,
    )


def column_of(row):
    return jnp.broadcast_to(row, (LANES, row.shape[1])).T


def kernel(cfg, sens_hbm, duals_ref, cov_ref, coords_ref, time_ref, owner_ref, out_ref, *s):
    n_hi, n_cell, gather, scatter = cfg
    n_tm = 2 * n_hi
    (sens, full, coords_all, mask_t, picked, row_b, col_b, own_b, ids, cov_k, adj, held, acc,
     core_out, core_in, x_out, x_in, total, cell_out, cell_in, local_sem, *pairs) = s
    co, ac, ax, ap, bx, bp, ring_r, ring_l, dp, dx, dc = zip(pairs[0::2], pairs[1::2])
    obs, cells = sens.shape
    rows = duals_ref.shape[0]
    half = cells // HALVES

    tm = lax.axis_index("tm")
    cell = lax.axis_index("cell")
    hi, core = tm // 2, tm % 2
    partner = (hi * 2 + (1 - core), cell)

    def hi_at(q):
        return lax.rem(hi + q + n_hi, n_hi)

    def x_peer(q):
        return (hi_at(q) * 2 + core, cell)

    def cell_at(k):
        return lax.rem(cell + k + n_cell, n_cell)

    load = pltpu.make_async_copy(sens_hbm, sens, local_sem)
    load.start()

    barrier = pltpu.get_barrier_semaphore()
    peers = [(tm, cell_at(k)) for k in range(1, n_cell)] + [x_peer(q) for q in range(1, n_hi)] + [partner]
    for peer in peers:
        pl.semaphore_signal(barrier, inc=1, device_id=peer, device_id_type=MESH)
    pl.semaphore_wait(barrier, len(peers))

    sent = []

    def go(copy):
        copy.start()
        sent.append(copy)
        return copy

    co_copies = {}
    for k in range(1, n_cell):
        co_copies[k] = go(remote(coords_ref, coords_all.at[cell], co, k, (tm, cell_at(k))))

    def block(t, c):
        return full.at[t * n_cell + c]

    cell_copies, x_copies, core_copies = {}, {}, {}

    def forward_x(src, k):
        for q in range(1, n_hi):
            x_copies[q, k] = go(remote(src, block(tm, cell_at(-k)), ax, q * n_cell + k, x_peer(q)))

    def forward_core(src, q, k):
        dst = block(hi_at(-q) * 2 + core, cell_at(-k))
        core_copies[q, k] = go(remote(src, dst, ap, q * n_cell + k, partner))

    if gather:
        for k in range(1, n_cell):
            cell_copies[k] = go(remote(duals_ref, block(tm, cell), ac, k, (tm, cell_at(k))))
        forward_x(duals_ref, 0)
        forward_core(duals_ref, 0, 0)
        full[tm * n_cell + cell] = duals_ref[...]

    coords_all[cell] = coords_ref[...]
    row_b[...] = column_of(coords_ref[0:1, :].astype(F32))
    col_b[...] = column_of(coords_ref[1:2, :].astype(F32))
    own_b[...] = column_of(owner_ref[...].astype(F32))
    live = tm <= time_ref[...]
    ids[...] = jnp.where(live, lax.broadcasted_iota(jnp.int32, (1, obs), 1), -1).astype(F32)

    def covariance_block(k):
        c = cell_at(-k)

        @pl.loop(0, cells // LANES)
        def _(j):
            lanes = pl.ds(pl.multiple_of(j * LANES, LANES), LANES)
            row_gap = row_b[...] - coords_all[c, 0:1, lanes].astype(F32)
            col_gap = col_b[...] - coords_all[c, 1:2, lanes].astype(F32)
            distance = jnp.sqrt(row_gap * row_gap + col_gap * col_gap)
            cov_k[c, :, lanes] = (jnp.exp(-distance / LSCALE) / (8.0 * LSCALE)).astype(BF16)

    def pick(i):
        at = slice(i * PICK_ROWS, (i + 1) * PICK_ROWS)
        owned = own_b[at, :]
        hot = [
            jnp.where(owned == ids[:, j * LANES:(j + 1) * LANES], 1.0, 0.0).astype(BF16)
            for j in range(obs // LANES)
        ]
        picked[at, :] = jnp.dot(
            jnp.concatenate(hot, axis=1), sens[...], preferred_element_type=F32
        ).astype(BF16)

    fillers = [functools.partial(pick, i) for i in range(obs // PICK_ROWS)]

    def fill():
        if fillers:
            fillers.pop(0)()

    covariance_block(0)
    load.wait()

    @pl.loop(0, obs // PICK_ROWS)
    def _(i):
        at = pl.ds(pl.multiple_of(i * PICK_ROWS, PICK_ROWS), PICK_ROWS)
        alive = jnp.where(ids[:, at] >= 0.0, 1.0, 0.0).astype(BF16)
        mask_t[:, at] = sens[at, :].T * alive

    for k in range(1, n_cell):
        if gather:
            cell_copies[k].wait_recv()
            src = block(tm, cell_at(-k))
            forward_x(src, k)
            forward_core(src, 0, k)
    if gather:
        for k in range(n_cell):
            for q in range(1, n_hi):
                x_copies[q, k].wait_recv()
                forward_core(block(hi_at(-q) * 2 + core, cell_at(-k)), q, k)
    for k in range(1, n_cell):
        co_copies[k].wait_recv()
        if k <= n_cell // 2:
            covariance_block(k)
    if gather:
        for k in range(n_cell):
            for q in range(n_hi):
                core_copies[q, k].wait_recv()

    bx_copies, bp_copies = {}, {}
    for h in range(HALVES):
        at = slice(h * half, (h + 1) * half)
        everything = full[...].reshape(obs, LANES) if gather else duals_ref[...]
        adj[tm, at, :] = jnp.dot(mask_t[at, :], everything, preferred_element_type=F32).astype(BF16)
        here = adj.at[tm, at]
        for q in range(1, n_hi):
            bx_copies[q, h] = go(remote(here, here, bx, q * HALVES + h, x_peer(q)))
        bp_copies[0, h] = go(remote(here, here, bp, h, partner))

    for k in range(n_cell // 2 + 1, n_cell):
        covariance_block(k)
    for h in range(HALVES):
        for q in range(1, n_hi):
            bx_copies[q, h].wait_recv()
            got = adj.at[hi_at(-q) * 2 + core, h * half:(h + 1) * half]
            bp_copies[q, h] = go(remote(got, got, bp, q * HALVES + h, partner))
    fill()

    major = cell // 2
    place = jnp.where(cell % 2 == 0, major, n_cell - 1 - major)

    def cell_on(k):
        p = lax.rem(place + k + n_cell, n_cell)
        return jnp.where(p < n_cell // 2, p * 2, (n_cell - 1 - p) * 2 + 1)

    steps = n_cell // 2
    ring = {}

    def carries(way, step, h):
        return step < steps or (step == steps and (h == 0 if way > 0 else h == 1))

    def ring_send(way, step, h):
        if carries(way, step, h):
            part = held.at[cell_on(-way * (step - 1)), h * half:(h + 1) * half]
            sems = ring_r if way > 0 else ring_l
            ring[way, step, h] = go(remote(part, part, sems, step * HALVES + h, (tm, cell_on(way))))

    for h in range(HALVES):
        at = slice(h * half, (h + 1) * half)
        for q in range(n_hi):
            bp_copies[q, h].wait_recv()
        mixed = cov_ref[tm, 0] * adj[0, at, :].astype(F32)
        for t in range(1, n_tm):
            mixed += cov_ref[tm, t] * adj[t, at, :].astype(F32)
        held[cell, at, :] = mixed.astype(BF16)
        ring_send(1, 1, h)
        ring_send(-1, 1, h)

    def spread(c):
        return jnp.dot(cov_k[c], held[c], preferred_element_type=F32)

    acc[...] = spread(cell)
    for step in range(1, steps + 1):
        for h in range(HALVES):
            for way in (1, -1):
                if carries(way, step, h):
                    ring[way, step, h].wait_recv()
                    ring_send(way, step + 1, h)
            fill()
        if step < steps:
            acc[...] += spread(cell_on(-step)) + spread(cell_on(step))
        else:
            acc[...] += spread(cell_on(step))
    while fillers:
        fill()

    weighted = acc[...].astype(BF16)
    if scatter:
        span = rows * n_cell

        def product(t):
            at = pl.ds(pl.multiple_of(t * span, span), span)
            return jnp.dot(picked[at, :], weighted, preferred_element_type=F32)

        dp_copies, dx_copies, dc_copies = {}, {}, {}
        order = [*range(1, n_hi), 0]
        for q in order:
            core_out[q] = product(hi_at(q) * 2 + (1 - core)).astype(BF16)
            dp_copies[q] = go(remote(core_out.at[q], core_in.at[q], dp, q, partner))
        for q in order:
            summed = product(hi_at(q) * 2 + core)
            dp_copies[q].wait_recv()
            summed += core_in[q].astype(F32)
            if q:
                x_out[q] = summed.astype(BF16)
                dx_copies[q] = go(remote(x_out.at[q], x_in.at[q], dx, q, x_peer(q)))
        for q in range(1, n_hi):
            dx_copies[q].wait_recv()
            summed += x_in[q].astype(F32)
        total[...] = summed.reshape(n_cell, rows, LANES)
        cell_out[...] = summed.astype(BF16).reshape(n_cell, rows, LANES)
        for k in range(1, n_cell):
            dc_copies[k] = go(remote(cell_out.at[cell_at(k)], cell_in.at[k], dc, k, (tm, cell_at(k))))
        result = total[cell]
        for k in range(1, n_cell):
            dc_copies[k].wait_recv()
            result += cell_in[k].astype(F32)
        out_ref[...] = result
    else:
        for i in range(obs // PICK_ROWS):
            at = slice(i * PICK_ROWS, (i + 1) * PICK_ROWS)
            out_ref[at, :] = jnp.dot(picked[at, :], weighted, preferred_element_type=F32)

    for copy in sent:
        copy.wait_send()


def per_device(n_tm, n_cell, sensitivity, duals, time_cov, cell_coords, obs_time, obs_owner):
    obs, _, cells = sensitivity.shape
    rows, reals = duals.shape
    n_hi = n_tm // 2
    inside = rows % 16 == 0
    if not inside:
        duals = lax.all_gather(duals, ("tm", "cell"), axis=0, tiled=True)
    span = rows * n_cell if inside else 16
    part = rows if inside else 16
    vmem = pl.BlockSpec(memory_space=pltpu.VMEM)

    def pair(count):
        return [pltpu.SemaphoreType.DMA((count,)), pltpu.SemaphoreType.DMA((count,))]

    steps = n_cell // 2 + 1
    out_rows = rows if inside else obs
    out = pl.pallas_call(
        functools.partial(kernel, (n_hi, n_cell, inside, inside)),
        out_shape=jax.ShapeDtypeStruct((out_rows, reals), F32),
        in_specs=[
            pl.BlockSpec(memory_space=pl.ANY), vmem, pl.BlockSpec(memory_space=pltpu.SMEM), vmem, vmem, vmem,
        ],
        out_specs=vmem,
        scratch_shapes=[
            pltpu.VMEM((obs, cells), BF16),
            pltpu.VMEM((n_tm * n_cell if inside else 1, part, reals), BF16),
            pltpu.VMEM((n_cell, 2, cells), jnp.int32),
            pltpu.VMEM((cells, obs), BF16),
            pltpu.VMEM((obs, cells), BF16),
            pltpu.VMEM((cells, LANES), F32),
            pltpu.VMEM((cells, LANES), F32),
            pltpu.VMEM((obs, LANES), F32),
            pltpu.VMEM((1, obs), F32),
            pltpu.VMEM((n_cell, cells, cells), BF16),
            pltpu.VMEM((n_tm, cells, reals), BF16),
            pltpu.VMEM((n_cell, cells, reals), BF16),
            pltpu.VMEM((cells, reals), F32),
            pltpu.VMEM((n_hi, span, reals), BF16),
            pltpu.VMEM((n_hi, span, reals), BF16),
            pltpu.VMEM((n_hi, span, reals), BF16),
            pltpu.VMEM((n_hi, span, reals), BF16),
            pltpu.VMEM((n_cell, part, reals), F32),
            pltpu.VMEM((n_cell, part, reals), BF16),
            pltpu.VMEM((n_cell, part, reals), BF16),
            pltpu.SemaphoreType.DMA,
            *pair(n_cell), *pair(n_cell), *pair(n_hi * n_cell), *pair(n_hi * n_cell),
            *pair(n_hi * HALVES), *pair(n_hi * HALVES),
            *pair(steps * HALVES), *pair(steps * HALVES),
            *pair(n_hi), *pair(n_hi), *pair(n_cell),
        ],
        compiler_params=pltpu.CompilerParams(
            collective_id=0, has_side_effects=True, vmem_limit_bytes=62 * 1024 * 1024
        ),
    )(
        sensitivity.reshape(obs, cells), duals, time_cov, cell_coords,
        obs_time.reshape(1, obs), obs_owner.reshape(1, obs),
    )
    if inside:
        return out
    return lax.psum_scatter(out, ("tm", "cell"), scatter_dimension=0, tiled=True)


def solution(mesh):
    in_specs = (P(None, "tm", "cell"), P(("tm", "cell"), None), P(), P(None, "cell"), P(), P())
    out_specs = P(("tm", "cell"), None)
    return jax.shard_map(
        functools.partial(per_device, mesh.shape["tm"], mesh.shape["cell"]),
        mesh=mesh, in_specs=in_specs, out_specs=out_specs, check_vma=False,
    )
```

```python
import functools

import jax
import jax.numpy as jnp
from jax import lax
from jax.experimental import pallas as pl
from jax.experimental.pallas import tpu as pltpu
from jax.sharding import PartitionSpec as P

LSCALE = 4
LANES = 128
HALVES = 2
PICK_ROWS = 256
QUARTERS = 4
FILL = (0, 3, 3, 1, 1)
MESH = pl.DeviceIdType.MESH
BF16 = jnp.bfloat16
F32 = jnp.float32


def remote(src, dst, sems, index, device):
    send, recv = sems
    return pltpu.make_async_remote_copy(
        src_ref=src, dst_ref=dst, send_sem=send.at[index], recv_sem=recv.at[index],
        device_id=device, device_id_type=MESH,
    )


def column_of(row):
    return jnp.broadcast_to(row, (LANES, row.shape[1])).T


def kernel(cfg, sens_hbm, duals_ref, cov_ref, coords_ref, time_ref, owner_ref, out_ref, *s):
    n_hi, n_cell, gather, scatter = cfg
    n_tm = 2 * n_hi
    (sens, full, coords_all, mask_t, picked, row_b, col_b, own_b, ids, cov_k, adj, held, acc,
     core_out, core_in, x_out, x_in, total, cell_out, cell_in, local_sem, *pairs) = s
    co, ac, ax, ap, bx, bp, ring_r, ring_l, dp, dx, dc = zip(pairs[0::2], pairs[1::2])
    obs, cells = sens.shape
    rows = duals_ref.shape[0]
    half = cells // HALVES
    quarter = cells // QUARTERS

    tm = lax.axis_index("tm")
    cell = lax.axis_index("cell")
    hi, core = tm // 2, tm % 2
    partner = (hi * 2 + (1 - core), cell)

    def hi_at(q):
        return lax.rem(hi + q + n_hi, n_hi)

    def x_peer(q):
        return (hi_at(q) * 2 + core, cell)

    def cell_at(k):
        return lax.rem(cell + k + n_cell, n_cell)

    load = pltpu.make_async_copy(sens_hbm, sens, local_sem)
    load.start()

    barrier = pltpu.get_barrier_semaphore()
    peers = [(tm, cell_at(k)) for k in range(1, n_cell)] + [x_peer(q) for q in range(1, n_hi)] + [partner]
    for peer in peers:
        pl.semaphore_signal(barrier, inc=1, device_id=peer, device_id_type=MESH)
    coords_all[cell] = coords_ref[...]
    row_b[...] = column_of(coords_ref[0:1, :].astype(F32))
    col_b[...] = column_of(coords_ref[1:2, :].astype(F32))
    own_b[...] = column_of(owner_ref[...].astype(F32))
    live = tm <= time_ref[...]
    ids[...] = jnp.where(live, lax.broadcasted_iota(jnp.int32, (1, obs), 1), -1).astype(F32)

    def covariance_block(c):
        @pl.loop(0, cells // LANES)
        def _(j):
            lanes = pl.ds(pl.multiple_of(j * LANES, LANES), LANES)
            row_gap = row_b[...] - coords_all[c, 0:1, lanes].astype(F32)
            col_gap = col_b[...] - coords_all[c, 1:2, lanes].astype(F32)
            distance = jnp.sqrt(row_gap * row_gap + col_gap * col_gap)
            cov_k[c, :, lanes] = (jnp.exp(-distance / LSCALE) / (8.0 * LSCALE)).astype(BF16)

    def pick(i):
        at = slice(i * PICK_ROWS, (i + 1) * PICK_ROWS)
        owned = own_b[at, :]
        hot = [
            jnp.where(owned == ids[:, j * LANES:(j + 1) * LANES], 1.0, 0.0).astype(BF16)
            for j in range(obs // LANES)
        ]
        picked[at, :] = jnp.dot(
            jnp.concatenate(hot, axis=1), sens[...], preferred_element_type=F32
        ).astype(BF16)

    fillers = [functools.partial(pick, i) for i in range(obs // PICK_ROWS)]

    def fill(count):
        for _ in range(count):
            if fillers:
                fillers.pop(0)()

    covariance_block(cell)
    load.wait()

    @pl.loop(0, obs // PICK_ROWS)
    def _(i):
        at = pl.ds(pl.multiple_of(i * PICK_ROWS, PICK_ROWS), PICK_ROWS)
        alive = jnp.where(ids[:, at] >= 0.0, 1.0, 0.0).astype(BF16)
        mask_t[:, at] = sens[at, :].T * alive

    fill(FILL[0])
    pl.semaphore_wait(barrier, len(peers))

    sent = []

    def go(copy):
        copy.start()
        sent.append(copy)
        return copy

    co_copies = {}
    for k in range(1, n_cell):
        co_copies[k] = go(remote(coords_ref, coords_all.at[cell], co, k, (tm, cell_at(k))))

    def block(t, c):
        return full.at[t * n_cell + c]

    cell_copies, x_copies, core_copies = {}, {}, {}

    def forward_x(src, k):
        for q in range(1, n_hi):
            x_copies[q, k] = go(remote(src, block(tm, cell_at(-k)), ax, q * n_cell + k, x_peer(q)))

    def forward_core(src, q, k):
        dst = block(hi_at(-q) * 2 + core, cell_at(-k))
        core_copies[q, k] = go(remote(src, dst, ap, q * n_cell + k, partner))

    if gather:
        for k in range(1, n_cell):
            cell_copies[k] = go(remote(duals_ref, block(tm, cell), ac, k, (tm, cell_at(k))))
        forward_x(duals_ref, 0)
        forward_core(duals_ref, 0, 0)
        full[tm * n_cell + cell] = duals_ref[...]

    fill(FILL[1])
    for k in range(1, n_cell):
        if gather:
            cell_copies[k].wait_recv()
            src = block(tm, cell_at(-k))
            forward_x(src, k)
            forward_core(src, 0, k)
    fill(FILL[2])
    if gather:
        for k in range(n_cell):
            for q in range(1, n_hi):
                x_copies[q, k].wait_recv()
                forward_core(block(hi_at(-q) * 2 + core, cell_at(-k)), q, k)
    for k in range(1, n_cell):
        co_copies[k].wait_recv()
    if gather:
        for k in range(n_cell):
            for q in range(n_hi):
                core_copies[q, k].wait_recv()

    bx_copies, bp_copies = {}, {}
    for h in range(HALVES):
        at = slice(h * half, (h + 1) * half)
        everything = full[...].reshape(obs, LANES) if gather else duals_ref[...]
        adj[tm, at, :] = jnp.dot(mask_t[at, :], everything, preferred_element_type=F32).astype(BF16)
        here = adj.at[tm, at]
        for q in range(1, n_hi):
            bx_copies[q, h] = go(remote(here, here, bx, q * HALVES + h, x_peer(q)))
        bp_copies[0, h] = go(remote(here, here, bp, h, partner))

    fill(FILL[3])
    for h in range(HALVES):
        for q in range(1, n_hi):
            bx_copies[q, h].wait_recv()
            got = adj.at[hi_at(-q) * 2 + core, h * half:(h + 1) * half]
            bp_copies[q, h] = go(remote(got, got, bp, q * HALVES + h, partner))
    fill(FILL[4])

    major = cell // 2
    place = jnp.where(cell % 2 == 0, major, n_cell - 1 - major)

    def cell_on(k):
        p = lax.rem(place + k + n_cell, n_cell)
        return jnp.where(p < n_cell // 2, p * 2, (n_cell - 1 - p) * 2 + 1)

    steps = n_cell // 2
    ring = {}

    def carries(way, step, h):
        return step < steps or (step == steps and (h < QUARTERS // 2) == (way > 0))

    def ring_send(way, step, h):
        if carries(way, step, h):
            part = held.at[cell_on(-way * (step - 1)), h * quarter:(h + 1) * quarter]
            sems = ring_r if way > 0 else ring_l
            ring[way, step, h] = go(remote(part, part, sems, step * QUARTERS + h, (tm, cell_on(way))))

    per_half = QUARTERS // HALVES
    for h in range(HALVES):
        at = slice(h * half, (h + 1) * half)
        for q in range(n_hi):
            bp_copies[q, h].wait_recv()
        mixed = cov_ref[tm, 0] * adj[0, at, :].astype(F32)
        for t in range(1, n_tm):
            mixed += cov_ref[tm, t] * adj[t, at, :].astype(F32)
        held[cell, at, :] = mixed.astype(BF16)
        for piece in range(h * per_half, (h + 1) * per_half):
            ring_send(1, 1, piece)
            ring_send(-1, 1, piece)

    def spread(c):
        return jnp.dot(cov_k[c], held[c], preferred_element_type=F32)

    def blocks(step):
        return [cell_on(-step), cell_on(step)] if step < steps else [cell_on(step)]

    acc[...] = spread(cell)
    for c in blocks(1):
        covariance_block(c)
    for step in range(1, steps + 1):
        for h in range(QUARTERS):
            for way in (1, -1):
                if carries(way, step, h):
                    ring[way, step, h].wait_recv()
                    ring_send(way, step + 1, h)
            if step < steps and h < len(blocks(step + 1)):
                covariance_block(blocks(step + 1)[h])
        for c in blocks(step):
            acc[...] += spread(c)
    fill(len(fillers))

    weighted = acc[...].astype(BF16)
    if scatter:
        span = rows * n_cell

        def product(t):
            at = pl.ds(pl.multiple_of(t * span, span), span)
            return jnp.dot(picked[at, :], weighted, preferred_element_type=F32)

        dp_copies, dx_copies, dc_copies = {}, {}, {}
        order = [*range(1, n_hi), 0]
        for q in order:
            core_out[q] = product(hi_at(q) * 2 + (1 - core)).astype(BF16)
            dp_copies[q] = go(remote(core_out.at[q], core_in.at[q], dp, q, partner))
        far = sorted(range(n_cell), key=lambda k: -min(k, n_cell - k))
        for q in order:
            summed = product(hi_at(q) * 2 + core)
            dp_copies[q].wait_recv()
            total[...] = (summed + core_in[q].astype(F32)).reshape(n_cell, rows, LANES)
            if q:
                for k in far:
                    c = cell_at(k)
                    x_out[q, c] = total[c].astype(BF16)
                    dx_copies[q, k] = go(remote(x_out.at[q, c], x_in.at[q, c], dx, q * n_cell + k, x_peer(q)))
        for k in far:
            c = cell_at(k)
            block_sum = total[c]
            for q in range(1, n_hi):
                dx_copies[q, k].wait_recv()
                block_sum += x_in[q, c].astype(F32)
            if k:
                cell_out[c] = block_sum.astype(BF16)
                dc_copies[k] = go(remote(cell_out.at[c], cell_in.at[k], dc, k, (tm, c)))
        result = block_sum
        for k in range(1, n_cell):
            dc_copies[k].wait_recv()
            result += cell_in[k].astype(F32)
        out_ref[...] = result
    else:
        for i in range(obs // PICK_ROWS):
            at = slice(i * PICK_ROWS, (i + 1) * PICK_ROWS)
            out_ref[at, :] = jnp.dot(picked[at, :], weighted, preferred_element_type=F32)

    for copy in sent:
        copy.wait_send()


def per_device(n_tm, n_cell, sensitivity, duals, time_cov, cell_coords, obs_time, obs_owner):
    obs, _, cells = sensitivity.shape
    rows, reals = duals.shape
    n_hi = n_tm // 2
    inside = rows % 16 == 0
    if not inside:
        duals = lax.all_gather(duals, ("tm", "cell"), axis=0, tiled=True)
    span = rows * n_cell if inside else 16
    part = rows if inside else 16
    vmem = pl.BlockSpec(memory_space=pltpu.VMEM)

    def pair(count):
        return [pltpu.SemaphoreType.DMA((count,)), pltpu.SemaphoreType.DMA((count,))]

    steps = n_cell // 2 + 1
    out_rows = rows if inside else obs
    out = pl.pallas_call(
        functools.partial(kernel, (n_hi, n_cell, inside, inside)),
        out_shape=jax.ShapeDtypeStruct((out_rows, reals), F32),
        in_specs=[
            pl.BlockSpec(memory_space=pl.ANY), vmem, pl.BlockSpec(memory_space=pltpu.SMEM), vmem, vmem, vmem,
        ],
        out_specs=vmem,
        scratch_shapes=[
            pltpu.VMEM((obs, cells), BF16),
            pltpu.VMEM((n_tm * n_cell if inside else 1, part, reals), BF16),
            pltpu.VMEM((n_cell, 2, cells), jnp.int32),
            pltpu.VMEM((cells, obs), BF16),
            pltpu.VMEM((obs, cells), BF16),
            pltpu.VMEM((cells, LANES), F32),
            pltpu.VMEM((cells, LANES), F32),
            pltpu.VMEM((obs, LANES), F32),
            pltpu.VMEM((1, obs), F32),
            pltpu.VMEM((n_cell, cells, cells), BF16),
            pltpu.VMEM((n_tm, cells, reals), BF16),
            pltpu.VMEM((n_cell, cells, reals), BF16),
            pltpu.VMEM((cells, reals), F32),
            pltpu.VMEM((n_hi, span, reals), BF16),
            pltpu.VMEM((n_hi, span, reals), BF16),
            pltpu.VMEM((n_hi, n_cell, part, reals), BF16),
            pltpu.VMEM((n_hi, n_cell, part, reals), BF16),
            pltpu.VMEM((n_cell, part, reals), F32),
            pltpu.VMEM((n_cell, part, reals), BF16),
            pltpu.VMEM((n_cell, part, reals), BF16),
            pltpu.SemaphoreType.DMA,
            *pair(n_cell), *pair(n_cell), *pair(n_hi * n_cell), *pair(n_hi * n_cell),
            *pair(n_hi * HALVES), *pair(n_hi * HALVES),
            *pair(steps * QUARTERS), *pair(steps * QUARTERS),
            *pair(n_hi), *pair(n_hi * n_cell), *pair(n_cell),
        ],
        compiler_params=pltpu.CompilerParams(
            collective_id=0, has_side_effects=True, vmem_limit_bytes=62 * 1024 * 1024
        ),
    )(
        sensitivity.reshape(obs, cells), duals, time_cov, cell_coords,
        obs_time.reshape(1, obs), obs_owner.reshape(1, obs),
    )
    if inside:
        return out
    return lax.psum_scatter(out, ("tm", "cell"), scatter_dimension=0, tiled=True)


def solution(mesh):
    in_specs = (P(None, "tm", "cell"), P(("tm", "cell"), None), P(), P(None, "cell"), P(), P())
    out_specs = P(("tm", "cell"), None)
    return jax.shard_map(
        functools.partial(per_device, mesh.shape["tm"], mesh.shape["cell"]),
        mesh=mesh, in_specs=in_specs, out_specs=out_specs, check_vma=False,
    )
```
